32 devices in a mesh: rep: 16 (over z, y, core), grp: 2 (over x).
Axes of the slice: x: 2, y: 2, z: 4, core: 2. Of those that a mesh axis runs over, the one named last changes fastest.
Arguments:
- tokens: bfloat16 [16, 256, 1024], P('rep', 'grp'), may hold values from -24 to 24
- cotangent: bfloat16 [16, 256, 1024], P('rep', 'grp'), may hold values from -6 to 6
- block_order: int32 [16, 4], P('rep'), may hold values from 0 to 3, each once within a row
- ln1_gain: float32 [1024], replicated, may hold values from 0.5 to 1.5
- ln1_bias: float32 [1024], replicated, may hold values from -1.5 to 1.5
- ln2_gain: float32 [1024], replicated, may hold values from 0.5 to 1.5
- ln2_bias: float32 [1024], replicated, may hold values from -1.5 to 1.5
- w_qkv: bfloat16 [1024, 3072], P('grp'), may hold values from -4 to 4
- qv_bias: float32 [2, 1024], replicated, may hold values from -1.5 to 1.5
- w_out: bfloat16 [1024, 1024], P('grp'), may hold values from -1.5 to 1.5
- w_fc1: bfloat16 [1024, 4096], P('grp'), may hold values from -0.1875 to 0.1875
- fc1_bias: float32 [4096], replicated, may hold values from -1.5 to 1.5
- w_fc2: bfloat16 [4096, 1024], P('grp'), may hold values from -0.09375 to 0.09375
- fc2_bias: float32 [1024], replicated, may hold values from -1.5 to 1.5
Outputs:
- output: bfloat16 [16, 256, 1024], P('rep', 'grp')
- input_grad: float32 [16, 256, 1024], P('rep', 'grp')
- ln1_gain_grad: float32 [1024], P('grp')
- ln1_bias_grad: float32 [1024], P('grp')
- ln2_gain_grad: float32 [1024], P('grp')
- ln2_bias_grad: float32 [1024], P('grp')
- qkv_grad: float32 [1024, 3072], P('grp')
- qv_bias_grad: float32 [2, 1024], P(None, 'grp')
- out_grad: float32 [1024, 1024], P('grp')
- fc1_grad: float32 [1024, 4096], P('grp')
- fc1_bias_grad: float32 [4096], P('grp')
- fc2_grad: float32 [4096, 1024], P('grp')
- fc2_bias_grad: float32 [1024], P('grp')
The draws below stay inside these ranges and needn't reach their ends.
Inputs may be any that keep to these rules, and one draw needn't show every extreme that they name: `block_order`: each row lists every block number once.
All inputs are finite; a program needn't handle non-finite values.
Results may differ from the reference program's by a relative error of at most 0.0087.
Values may be sent and summed in bfloat16 or wider, within the bound.
A program may use at most 256 MiB of HBM per device.

```python
import math
import jax
import jax.numpy as jnp
from jax import lax

D = 1024
HEADS = 16
HEAD = 64
ROT = 16
FF = 4096
BLOCK = 64
BLOCKS = 4
LEN = 256
SEQS = 16


def draw_tokens(key, part):
    key_core, key_rows, key_cols = jax.random.split(key, 3)
    core = jnp.clip(jax.random.normal(key_core, (SEQS, LEN, D), jnp.float32), -4.0, 4.0)
    rows_scale = jnp.exp(jax.random.uniform(key_rows, (SEQS, LEN, 1), jnp.float32, math.log(0.3), math.log(3.0)))
    cols_scale = jnp.exp(jax.random.uniform(key_cols, (1, 1, D), jnp.float32, math.log(0.5), math.log(2.0)))
    return (core * rows_scale * cols_scale).astype(jnp.bfloat16)


def draw_w_qkv(key, part):
    key_base = jax.random.fold_in(key, 0)
    base = jnp.clip(jax.random.normal(key_base, (D, 3 * D), jnp.float32), -5.0, 5.0) / math.sqrt(D)
    return base.astype(jnp.bfloat16)


def block_levels(key, dims, cuts, least, largest):
    factor_of, own = 1.0, jax.random.fold_in(key, 6)
    for position, blocks in cuts:
        heights = jnp.exp(jax.random.uniform(jax.random.fold_in(own, position), (blocks,), jnp.float32, least / len(cuts), largest / len(cuts)))
        factor_of = factor_of * jnp.repeat(heights, dims[position] // blocks).reshape([-1 if axis == position else 1 for axis in range(len(dims))])
    return factor_of


def centred(stream_key, shape, scale, most, cuts=(), kind=jnp.bfloat16):
    values = jax.random.normal(stream_key, shape, jnp.float32) * scale
    if len(cuts) > 0:
        values = block_levels(stream_key, shape, cuts, -0.22, 0.18) * values
    return jnp.clip(values, min=-most, max=most).astype(kind)


def setup_inputs(seed: int = 0) -> dict:
    key_list = jax.random.split(jax.random.key(seed), 15)
    tokens = draw_tokens(jax.random.fold_in(key_list[14], 71), 0)
    cotangent = centred(key_list[1], (SEQS, LEN, D), 1.0, 6.0, ((0, 16), (1, 2)))
    block_order = jax.vmap(lambda own: jax.random.permutation(own, BLOCKS))(jax.random.split(key_list[2], SEQS)).reshape((SEQS, BLOCKS)).astype(jnp.int32)
    ln1_gain = jnp.clip(1.0 + 0.1 * jax.random.normal(key_list[3], (D,), jnp.float32), 0.5, 1.5)
    ln1_bias = centred(key_list[4], (D,), 0.3, 1.5, (), jnp.float32)
    ln2_gain = jnp.clip(1.0 + 0.1 * jax.random.normal(key_list[5], (D,), jnp.float32), 0.5, 1.5)
    ln2_bias = centred(key_list[6], (D,), 0.3, 1.5, (), jnp.float32)
    w_qkv = draw_w_qkv(jax.random.fold_in(key_list[14], 71), 0)
    qv_bias = centred(key_list[8], (2, D), 0.3, 1.5, (), jnp.float32)
    w_out = centred(key_list[9], (D, D), (D // 64) ** -0.5, 1.5, ((0, 2),))
    w_fc1 = centred(key_list[10], (D, FF), D ** -0.5, 0.1875, ((0, 2),))
    fc1_bias = centred(key_list[11], (FF,), 0.3, 1.5, (), jnp.float32)
    w_fc2 = centred(key_list[12], (FF, D), FF ** -0.5, 0.09375, ((0, 2),))
    fc2_bias = centred(key_list[13], (D,), 0.3, 1.5, (), jnp.float32)
    return dict(tokens=tokens, cotangent=cotangent, block_order=block_order, ln1_gain=ln1_gain, ln1_bias=ln1_bias, ln2_gain=ln2_gain, ln2_bias=ln2_bias, w_qkv=w_qkv, qv_bias=qv_bias, w_out=w_out, w_fc1=w_fc1, fc1_bias=fc1_bias, w_fc2=w_fc2, fc2_bias=fc2_bias)


EPS = 1e-05
NEGATIVE = -1e+30

def rotary_tables(positions):
    half = ROT // 2
    frequency = 10000.0 ** (-jnp.arange(half, dtype=jnp.float32) * (2.0 / ROT))
    angles = positions.astype(jnp.float32)[:, None] * frequency[None, :]
    return (jnp.cos(angles)[:, None, :], jnp.sin(angles)[:, None, :])

def rotate(values, cosine, sine):
    half = ROT // 2
    first_half = values[..., :half]
    second_half = values[..., half:ROT]
    return jnp.concatenate([first_half * cosine - second_half * sine, second_half * cosine + first_half * sine, values[..., ROT:]], -1)

def unrotate(values, cosine, sine):
    half = ROT // 2
    first_half = values[..., :half]
    second_half = values[..., half:ROT]
    return jnp.concatenate([first_half * cosine + second_half * sine, second_half * cosine - first_half * sine, values[..., ROT:]], -1)

def norm_forward(inputs, gain, shift):
    centre = inputs - lax.optimization_barrier(jnp.mean(inputs, -1, keepdims=True))
    scale_inv = lax.rsqrt(lax.optimization_barrier(jnp.mean(centre * centre, -1, keepdims=True)) + EPS)
    normed = centre * scale_inv
    return (normed, scale_inv, (normed * gain + shift).astype(jnp.bfloat16))

def norm_backward(upstream, normed, scale_inv, gain):
    scaled = upstream * gain
    return scale_inv * (scaled - lax.optimization_barrier(jnp.mean(scaled, -1, keepdims=True)) - normed * lax.optimization_barrier(jnp.mean(scaled * normed, -1, keepdims=True)))

def gelu_exact(hidden):
    return 0.5 * hidden * (1.0 + lax.erf(hidden * 0.7071067811865476))

def gelu_slope(hidden):
    return 0.5 * (1.0 + lax.erf(hidden * 0.7071067811865476)) + hidden * jnp.exp(-0.5 * hidden * hidden) * 0.3989422804014327

def reference(tokens, cotangent, block_order, ln1_gain, ln1_bias, ln2_gain, ln2_bias, w_qkv, qv_bias, w_out, w_fc1, fc1_bias, w_fc2, fc2_bias):
    score_scale = HEAD ** (-0.5)

    def one_sequence(totals, item):
        tokens_seq, upstream, block_list = item
        row_ids = jnp.arange(LEN, dtype=jnp.int32)
        positions = block_list[row_ids // BLOCK] * BLOCK + row_ids % BLOCK
        cosine, sine = rotary_tables(positions)
        inputs = tokens_seq.astype(jnp.float32)
        normed_one, rstd_one, scaled_one = norm_forward(inputs, ln1_gain, ln1_bias)
        normed_two, rstd_two, scaled_two = norm_forward(inputs, ln2_gain, ln2_bias)
        qkv = jnp.dot(scaled_one, w_qkv, preferred_element_type=jnp.float32)
        query = (qkv[:, :D] + qv_bias[0]).reshape(LEN, HEADS, HEAD)
        keys = qkv[:, D:2 * D].reshape(LEN, HEADS, HEAD)
        value_b = (qkv[:, 2 * D:] + qv_bias[1]).astype(jnp.bfloat16).reshape(LEN, HEADS, HEAD)
        query_b = rotate(query, cosine, sine).astype(jnp.bfloat16)
        keys_b = rotate(keys, cosine, sine).astype(jnp.bfloat16)
        allowed = positions[None, :, None] >= positions[None, None, :]
        raw = jnp.einsum('qhd,khd->hqk', query_b.astype(jnp.float32), keys_b.astype(jnp.float32)) * score_scale
        scores = jnp.where(allowed, raw, NEGATIVE)
        highest = lax.optimization_barrier(jnp.max(scores, -1, keepdims=True))
        log_total = highest + jnp.log(lax.optimization_barrier(jnp.sum(jnp.exp(scores - highest), -1, keepdims=True)))
        prob_f = jnp.exp(scores - log_total)
        prob_b = prob_f.astype(jnp.bfloat16)
        mixed = jnp.einsum('hqk,khd->qhd', prob_b.astype(jnp.float32), value_b.astype(jnp.float32)).astype(jnp.bfloat16).reshape(LEN, D)
        attn_branch = jnp.dot(mixed, w_out, preferred_element_type=jnp.float32)
        hidden = jnp.dot(scaled_two, w_fc1, preferred_element_type=jnp.float32) + fc1_bias
        act_b = gelu_exact(hidden).astype(jnp.bfloat16)
        mlp_branch = jnp.dot(act_b, w_fc2, preferred_element_type=jnp.float32)
        result = (inputs + attn_branch + mlp_branch + fc2_bias).astype(jnp.bfloat16)
        upstream_f = upstream.astype(jnp.float32)
        down_g = jnp.dot(act_b.T, upstream, preferred_element_type=jnp.float32)
        proj_g = jnp.dot(mixed.T, upstream, preferred_element_type=jnp.float32)
        d_hidden = jnp.dot(upstream, w_fc2.T, preferred_element_type=jnp.float32) * gelu_slope(hidden)
        d_hidden_b = d_hidden.astype(jnp.bfloat16)
        up_g = jnp.dot(scaled_two.T, d_hidden_b, preferred_element_type=jnp.float32)
        d_two = jnp.dot(d_hidden_b, w_fc1.T, preferred_element_type=jnp.float32)
        d_mixed = jnp.dot(upstream, w_out.T, preferred_element_type=jnp.float32).astype(jnp.bfloat16).reshape(LEN, HEADS, HEAD)
        d_value = jnp.einsum('hqk,qhd->khd', prob_b.astype(jnp.float32), d_mixed.astype(jnp.float32))
        d_prob = jnp.einsum('qhd,khd->hqk', d_mixed.astype(jnp.float32), value_b.astype(jnp.float32))
        delta = lax.optimization_barrier(jnp.sum(prob_f * d_prob, -1, keepdims=True))
        d_score = (prob_f * (d_prob - delta) * score_scale).astype(jnp.bfloat16)
        d_query = jnp.einsum('hqk,khd->qhd', d_score.astype(jnp.float32), keys_b.astype(jnp.float32))
        d_keys = jnp.einsum('hqk,qhd->khd', d_score.astype(jnp.float32), query_b.astype(jnp.float32))
        d_query = unrotate(d_query, cosine, sine).reshape(LEN, D)
        d_keys = unrotate(d_keys, cosine, sine).reshape(LEN, D)
        d_value = d_value.reshape(LEN, D)
        d_qkv = jnp.concatenate([d_query, d_keys, d_value], 1).astype(jnp.bfloat16)
        qkv_g = jnp.dot(scaled_one.T, d_qkv, preferred_element_type=jnp.float32)
        d_one = jnp.dot(d_qkv, w_qkv.T, preferred_element_type=jnp.float32)
        grad_in = upstream_f + norm_backward(d_one, normed_one, rstd_one, ln1_gain) + norm_backward(d_two, normed_two, rstd_two, ln2_gain)
        terms = (lax.optimization_barrier(jnp.sum(d_one * normed_one, 0)), lax.optimization_barrier(jnp.sum(d_one, 0)), lax.optimization_barrier(jnp.sum(d_two * normed_two, 0)), lax.optimization_barrier(jnp.sum(d_two, 0)), qkv_g, jnp.stack([lax.optimization_barrier(jnp.sum(d_query, 0)), lax.optimization_barrier(jnp.sum(d_value, 0))]), proj_g, up_g, lax.optimization_barrier(jnp.sum(d_hidden, 0)), down_g, lax.optimization_barrier(jnp.sum(upstream_f, 0)))
        totals = tuple((total + term for total, term in zip(totals, terms)))
        return (totals, (result, grad_in))
    float_type = jnp.float32
    start_totals = (jnp.zeros((D,), float_type), jnp.zeros((D,), float_type), jnp.zeros((D,), float_type), jnp.zeros((D,), float_type), jnp.zeros((D, 3 * D), float_type), jnp.zeros((2, D), float_type), jnp.zeros((D, D), float_type), jnp.zeros((D, FF), float_type), jnp.zeros((FF,), float_type), jnp.zeros((FF, D), float_type), jnp.zeros((D,), float_type))
    totals, (results, grads_in) = lax.scan(one_sequence, start_totals, (tokens, cotangent, block_order))
    return (results, grads_in, totals[0], totals[1], totals[2], totals[3], totals[4], totals[5], totals[6], totals[7], totals[8], totals[9], totals[10])
```

```python
import jax
import jax.numpy as jnp
from jax import lax
from jax.sharding import PartitionSpec as P

D = 1024
HEADS = 16
HEAD = 64
ROT = 16


EPS = 1e-05
NEGATIVE = -1e30


def rotary_tables(positions):
    half = ROT // 2
    frequency = 10000.0 ** (-jnp.arange(half, dtype=jnp.float32) * (2.0 / ROT))
    angles = positions.astype(jnp.float32)[:, None] * frequency[None, :]
    return (jnp.cos(angles)[:, None, :], jnp.sin(angles)[:, None, :])


def rotate(values, cosine, sine):
    half = ROT // 2
    first_half = values[..., :half]
    second_half = values[..., half:ROT]
    return jnp.concatenate(
        [
            first_half * cosine - second_half * sine,
            second_half * cosine + first_half * sine,
            values[..., ROT:],
        ],
        -1,
    )


def unrotate(values, cosine, sine):
    half = ROT // 2
    first_half = values[..., :half]
    second_half = values[..., half:ROT]
    return jnp.concatenate(
        [
            first_half * cosine + second_half * sine,
            second_half * cosine - first_half * sine,
            values[..., ROT:],
        ],
        -1,
    )


def gelu_exact(hidden):
    return 0.5 * hidden * (1.0 + lax.erf(hidden * 0.7071067811865476))


def gelu_slope(hidden):
    return (
        0.5 * (1.0 + lax.erf(hidden * 0.7071067811865476))
        + hidden * jnp.exp(-0.5 * hidden * hidden) * 0.3989422804014327
    )


def contract_last(left, right):
    return lax.dot_general(
        left, right, (((1,), (1,)), ((), ())), preferred_element_type=jnp.float32
    )


def contract_first(left, right):
    return lax.dot_general(
        left, right, (((0,), (0,)), ((), ())), preferred_element_type=jnp.float32
    )


def shift(value, distance):
    size = lax.axis_size("grp")
    return lax.ppermute(value, "grp", [(i, (i + distance) % size) for i in range(size)])


def gather_along(value, axis):
    size = lax.axis_size("grp")
    member = lax.axis_index("grp")
    width = value.shape[axis]
    shape = list(value.shape)
    shape[axis] = width * size
    whole = jnp.zeros(shape, value.dtype)
    for step in range(size):
        block = value if step == 0 else shift(value, step)
        owner = (member - step) % size
        whole = lax.dynamic_update_slice_in_dim(whole, block, owner * width, axis)
    return whole


def scatter_sum(part_for):
    size = lax.axis_size("grp")
    member = lax.axis_index("grp")
    arrived = []
    for step in range(1, size):
        term = part_for((member + step) % size)
        arrived.append(shift(term.astype(jnp.bfloat16), step))
    total = part_for(member)
    for term in arrived:
        total = total + term.astype(jnp.float32)
    return total


def columns_of(value, owner, width):
    return lax.dynamic_slice_in_dim(value, owner * width, width, value.ndim - 1)


def rows_of(value, owner, width):
    return lax.dynamic_slice_in_dim(value, owner * width, width, 0)


def rep_sum(values):
    return lax.psum([value.astype(jnp.bfloat16) for value in values], "rep")


def body(
    tokens,
    cotangent,
    block_order,
    ln1_gain,
    ln1_bias,
    ln2_gain,
    ln2_bias,
    w_qkv,
    qv_bias,
    w_out,
    w_fc1,
    fc1_bias,
    w_fc2,
    fc2_bias,
):
    float_type = jnp.float32
    half_type = jnp.bfloat16
    group_size = lax.axis_size("grp")
    member = lax.axis_index("grp")
    tok_count = tokens.shape[1]
    seq_total = tok_count * group_size
    block_size = tok_count // 2
    own_width = D // group_size
    own_heads = HEADS // group_size
    own_hidden = w_fc2.shape[0]
    score_scale = HEAD ** (-0.5)

    pair = gather_along(jnp.concatenate([tokens[0], cotangent[0]], 1), 0)
    inputs_b = pair[:, :D]
    upstream = pair[:, D:]
    row_ids = jnp.arange(seq_total, dtype=jnp.int32)
    block_ids = jnp.arange(2 * group_size, dtype=jnp.int32)
    matches = (row_ids // block_size)[:, None] == block_ids[None, :]
    all_pos = (
        jnp.sum(jnp.where(matches, block_order[0][None, :], 0), 1) * block_size
        + row_ids % block_size
    )
    cosine, sine = rotary_tables(all_pos)

    inputs = inputs_b.astype(float_type)
    centre = inputs - jnp.mean(inputs, -1, keepdims=True)
    rstd = lax.rsqrt(jnp.mean(centre * centre, -1, keepdims=True) + EPS)
    normed_cols = columns_of(inputs, member, own_width)
    normed_cols = (normed_cols - jnp.mean(inputs, -1, keepdims=True)) * rstd
    gain_one = columns_of(ln1_gain, member, own_width)
    gain_two = columns_of(ln2_gain, member, own_width)
    one_cols = (normed_cols * gain_one + columns_of(ln1_bias, member, own_width)).astype(half_type)
    two_cols = (normed_cols * gain_two + columns_of(ln2_bias, member, own_width)).astype(half_type)

    hidden = scatter_sum(
        lambda owner: jnp.dot(
            two_cols, columns_of(w_fc1, owner, own_hidden), preferred_element_type=float_type
        )
    )
    hidden = hidden + columns_of(fc1_bias, member, own_hidden)

    def qkv_part(owner):
        return jnp.concatenate(
            [
                jnp.dot(
                    one_cols,
                    columns_of(w_qkv[:, i * D : (i + 1) * D], owner, own_width),
                    preferred_element_type=float_type,
                )
                for i in range(3)
            ],
            1,
        )

    d_act = contract_last(upstream, w_fc2)
    d_mixed_b = contract_last(upstream, w_out).astype(half_type)
    act_b = gelu_exact(hidden).astype(half_type)
    d_hidden = d_act * gelu_slope(hidden)
    d_hidden_b = d_hidden.astype(half_type)
    down_part = contract_first(act_b, upstream).astype(half_type)
    hidden_group = gather_along(d_hidden_b, 1)
    qkv = scatter_sum(qkv_part)
    up_part = contract_first(two_cols, hidden_group).astype(half_type)
    d_two = contract_last(hidden_group, w_fc1)

    split = (seq_total, own_heads, HEAD)
    q_bias = columns_of(qv_bias[0], member, own_width)
    v_bias = columns_of(qv_bias[1], member, own_width)
    query = (qkv[:, :own_width] + q_bias).reshape(split)
    keys = qkv[:, own_width : 2 * own_width].reshape(split)
    value_b = (qkv[:, 2 * own_width :] + v_bias).astype(half_type).reshape(split)
    query_b = rotate(query, cosine, sine).astype(half_type)
    keys_b = rotate(keys, cosine, sine).astype(half_type)
    d_mixed_h = d_mixed_b.reshape(split)
    allowed = all_pos[None, :, None] >= all_pos[None, None, :]
    raw = (
        jnp.einsum("qhd,khd->hqk", query_b, keys_b, preferred_element_type=float_type)
        * score_scale
    )
    scores = jnp.where(allowed, raw, NEGATIVE)
    highest = jnp.max(scores, -1, keepdims=True)
    log_total = highest + jnp.log(jnp.sum(jnp.exp(scores - highest), -1, keepdims=True))
    prob_f = jnp.exp(scores - log_total)
    prob_b = prob_f.astype(half_type)
    mixed = (
        jnp.einsum("hqk,khd->qhd", prob_b, value_b, preferred_element_type=float_type)
        .astype(half_type)
        .reshape(seq_total, own_width)
    )
    proj_part = contract_first(mixed, upstream)
    d_prob = jnp.einsum("qhd,khd->hqk", d_mixed_h, value_b, preferred_element_type=float_type)
    delta = jnp.sum(prob_f * d_prob, -1, keepdims=True)
    d_score = (prob_f * (d_prob - delta) * score_scale).astype(half_type)
    d_query = jnp.einsum("hqk,khd->qhd", d_score, keys_b, preferred_element_type=float_type)
    d_query = unrotate(d_query, cosine, sine).reshape(seq_total, own_width)
    d_keys = jnp.einsum("hqk,qhd->khd", d_score, query_b, preferred_element_type=float_type)
    d_keys = unrotate(d_keys, cosine, sine).reshape(seq_total, own_width)
    d_value = jnp.einsum("hqk,qhd->khd", prob_b, d_mixed_h, preferred_element_type=float_type)
    d_value = d_value.reshape(seq_total, own_width)

    d_own = jnp.concatenate([d_query, d_keys, d_value], 1).astype(half_type)
    qkv_group = jnp.zeros((seq_total, 3 * D), half_type)
    for step in range(group_size):
        block = d_own if step == 0 else shift(d_own, step)
        owner = (member - step) % group_size
        for i in range(3):
            qkv_group = lax.dynamic_update_slice_in_dim(
                qkv_group,
                block[:, i * own_width : (i + 1) * own_width],
                i * D + owner * own_width,
                1,
            )
    qkv_part_grad = contract_first(one_cols, qkv_group)
    d_one = contract_last(qkv_group, w_qkv)

    branch_whole = jnp.dot(mixed, w_out, preferred_element_type=float_type) + jnp.dot(
        act_b, w_fc2, preferred_element_type=float_type
    )
    branches = scatter_sum(lambda owner: rows_of(branch_whole, owner, tok_count))
    result = (tokens[0].astype(float_type) + branches + fc2_bias).astype(half_type)

    small = jnp.concatenate(
        [
            jnp.sum(d_one * normed_cols, 0),
            jnp.sum(d_one, 0),
            jnp.sum(d_two * normed_cols, 0),
            jnp.sum(d_two, 0),
            jnp.sum(d_query, 0),
            jnp.sum(d_value, 0),
            jnp.sum(columns_of(upstream, member, own_width).astype(float_type), 0),
            jnp.sum(d_hidden, 0),
        ]
    )
    used = small.shape[0]
    small = jnp.pad(small, (0, -used % (16 * D))).reshape(-1, D)
    proj_part = jnp.concatenate([proj_part, small]).astype(half_type)
    down_grad, up_grad, qkv_grad, proj_grad = rep_sum(
        [down_part, up_part, qkv_part_grad, proj_part]
    )
    small = proj_grad[own_width:].astype(float_type).reshape(-1)[:used]
    proj_grad = proj_grad[:own_width]
    pieces = [small[i * own_width : (i + 1) * own_width] for i in range(7)]

    scaled = d_one * gain_one + d_two * gain_two
    scaled_rows = jnp.zeros((tok_count, D), float_type)
    for step in range(group_size):
        block = rows_of(scaled, (member + step) % group_size, tok_count)
        if step > 0:
            block = shift(block, step)
        owner = (member - step) % group_size
        scaled_rows = lax.dynamic_update_slice_in_dim(scaled_rows, block, owner * own_width, 1)
    own_inputs = tokens[0].astype(float_type)
    own_centre = own_inputs - jnp.mean(own_inputs, -1, keepdims=True)
    own_rstd = lax.rsqrt(jnp.mean(own_centre * own_centre, -1, keepdims=True) + EPS)
    own_normed = own_centre * own_rstd
    grad_in = cotangent[0].astype(float_type) + own_rstd * (
        scaled_rows
        - jnp.mean(scaled_rows, -1, keepdims=True)
        - own_normed * jnp.mean(scaled_rows * own_normed, -1, keepdims=True)
    )
    return (
        result[None],
        grad_in[None],
        pieces[0],
        pieces[1],
        pieces[2],
        pieces[3],
        qkv_grad.astype(float_type),
        jnp.stack([pieces[4], pieces[5]]),
        proj_grad.astype(float_type),
        up_grad.astype(float_type),
        small[7 * own_width :],
        down_grad.astype(float_type),
        pieces[6],
    )


def solution(mesh):
    placed = (
        P("rep", "grp", None),
        P("rep", "grp", None),
        P("rep", None),
        P(),
        P(),
        P(),
        P(),
        P("grp", None),
        P(),
        P("grp", None),
        P("grp", None),
        P(),
        P("grp", None),
        P(),
    )
    return jax.shard_map(
        body,
        mesh=mesh,
        in_specs=placed,
        out_specs=(
            P("rep", "grp", None),
            P("rep", "grp", None),
            P("grp"),
            P("grp"),
            P("grp"),
            P("grp"),
            P("grp", None),
            P(None, "grp"),
            P("grp", None),
            P("grp", None),
            P("grp"),
            P("grp", None),
            P("grp"),
        ),
        check_vma=False,
    )
```

```python
import jax
import jax.numpy as jnp
from jax import lax
from jax.sharding import PartitionSpec as P

D = 1024
HEADS = 16
HEAD = 64
ROT = 16


EPS = 1e-05
NEGATIVE = -1e30


def rotary_tables(positions):
    half = ROT // 2
    frequency = 10000.0 ** (-jnp.arange(half, dtype=jnp.float32) * (2.0 / ROT))
    angles = positions.astype(jnp.float32)[:, None] * frequency[None, :]
    return (jnp.cos(angles)[:, None, :], jnp.sin(angles)[:, None, :])


def rotate(values, cosine, sine):
    half = ROT // 2
    first_half = values[..., :half]
    second_half = values[..., half:ROT]
    return jnp.concatenate(
        [
            first_half * cosine - second_half * sine,
            second_half * cosine + first_half * sine,
            values[..., ROT:],
        ],
        -1,
    )


def unrotate(values, cosine, sine):
    half = ROT // 2
    first_half = values[..., :half]
    second_half = values[..., half:ROT]
    return jnp.concatenate(
        [
            first_half * cosine + second_half * sine,
            second_half * cosine - first_half * sine,
            values[..., ROT:],
        ],
        -1,
    )


def gelu_exact(hidden):
    return 0.5 * hidden * (1.0 + lax.erf(hidden * 0.7071067811865476))


def gelu_slope(hidden):
    return (
        0.5 * (1.0 + lax.erf(hidden * 0.7071067811865476))
        + hidden * jnp.exp(-0.5 * hidden * hidden) * 0.3989422804014327
    )


def contract_last(left, right):
    return lax.dot_general(
        left, right, (((1,), (1,)), ((), ())), preferred_element_type=jnp.float32
    )


def contract_first(left, right):
    return lax.dot_general(
        left, right, (((0,), (0,)), ((), ())), preferred_element_type=jnp.float32
    )


def shift(value, distance):
    size = lax.axis_size("grp")
    return lax.ppermute(value, "grp", [(i, (i + distance) % size) for i in range(size)])


def gather_along(value, axis):
    size = lax.axis_size("grp")
    member = lax.axis_index("grp")
    width = value.shape[axis]
    shape = list(value.shape)
    shape[axis] = width * size
    whole = jnp.zeros(shape, value.dtype)
    for step in range(size):
        block = value if step == 0 else shift(value, step)
        owner = (member - step) % size
        whole = lax.dynamic_update_slice_in_dim(whole, block, owner * width, axis)
    return whole


def scatter_sum(part_for):
    size = lax.axis_size("grp")
    member = lax.axis_index("grp")
    arrived = []
    for step in range(1, size):
        term = part_for((member + step) % size)
        arrived.append(shift(term.astype(jnp.bfloat16), step))
    total = part_for(member)
    for term in arrived:
        total = total + term.astype(jnp.float32)
    return total


def columns_of(value, owner, width):
    return lax.dynamic_slice_in_dim(value, owner * width, width, value.ndim - 1)


def rows_of(value, owner, width):
    return lax.dynamic_slice_in_dim(value, owner * width, width, 0)


def rep_sum(value):
    return lax.psum(value.astype(jnp.bfloat16), "rep")


def body(
    tokens,
    cotangent,
    block_order,
    ln1_gain,
    ln1_bias,
    ln2_gain,
    ln2_bias,
    w_qkv,
    qv_bias,
    w_out,
    w_fc1,
    fc1_bias,
    w_fc2,
    fc2_bias,
):
    float_type = jnp.float32
    half_type = jnp.bfloat16
    group_size = lax.axis_size("grp")
    member = lax.axis_index("grp")
    tok_count = tokens.shape[1]
    seq_total = tok_count * group_size
    block_size = tok_count // 2
    own_width = D // group_size
    own_heads = HEADS // group_size
    own_hidden = w_fc2.shape[0]
    score_scale = HEAD ** (-0.5)

    pair = gather_along(jnp.concatenate([tokens[0], cotangent[0]], 1), 0)
    inputs_b = pair[:, :D]
    upstream = pair[:, D:]
    row_ids = jnp.arange(seq_total, dtype=jnp.int32)
    block_ids = jnp.arange(2 * group_size, dtype=jnp.int32)
    matches = (row_ids // block_size)[:, None] == block_ids[None, :]
    all_pos = (
        jnp.sum(jnp.where(matches, block_order[0][None, :], 0), 1) * block_size
        + row_ids % block_size
    )
    cosine, sine = rotary_tables(all_pos)

    inputs = inputs_b.astype(float_type)
    centre = inputs - jnp.mean(inputs, -1, keepdims=True)
    rstd = lax.rsqrt(jnp.mean(centre * centre, -1, keepdims=True) + EPS)
    normed_cols = columns_of(inputs, member, own_width)
    normed_cols = (normed_cols - jnp.mean(inputs, -1, keepdims=True)) * rstd
    gain_one = columns_of(ln1_gain, member, own_width)
    gain_two = columns_of(ln2_gain, member, own_width)
    one_cols = (normed_cols * gain_one + columns_of(ln1_bias, member, own_width)).astype(half_type)
    two_cols = (normed_cols * gain_two + columns_of(ln2_bias, member, own_width)).astype(half_type)

    hidden = scatter_sum(
        lambda owner: jnp.dot(
            two_cols, columns_of(w_fc1, owner, own_hidden), preferred_element_type=float_type
        )
    )
    hidden = hidden + columns_of(fc1_bias, member, own_hidden)

    def qkv_part(owner):
        return jnp.concatenate(
            [
                jnp.dot(
                    one_cols,
                    columns_of(w_qkv[:, i * D : (i + 1) * D], owner, own_width),
                    preferred_element_type=float_type,
                )
                for i in range(3)
            ],
            1,
        )

    d_act = contract_last(upstream, w_fc2)
    d_mixed_b = contract_last(upstream, w_out).astype(half_type)
    act_b = gelu_exact(hidden).astype(half_type)
    d_hidden = d_act * gelu_slope(hidden)
    d_hidden_b = d_hidden.astype(half_type)
    down_grad = rep_sum(contract_first(act_b, upstream))
    hidden_group = gather_along(d_hidden_b, 1)
    qkv = scatter_sum(qkv_part)
    up_grad = rep_sum(contract_first(two_cols, hidden_group))
    d_two = contract_last(hidden_group, w_fc1)

    split = (seq_total, own_heads, HEAD)
    q_bias = columns_of(qv_bias[0], member, own_width)
    v_bias = columns_of(qv_bias[1], member, own_width)
    query = (qkv[:, :own_width] + q_bias).reshape(split)
    keys = qkv[:, own_width : 2 * own_width].reshape(split)
    value_b = (qkv[:, 2 * own_width :] + v_bias).astype(half_type).reshape(split)
    query_b = rotate(query, cosine, sine).astype(half_type)
    keys_b = rotate(keys, cosine, sine).astype(half_type)
    d_mixed_h = d_mixed_b.reshape(split)
    allowed = all_pos[None, :, None] >= all_pos[None, None, :]
    raw = (
        jnp.einsum("qhd,khd->hqk", query_b, keys_b, preferred_element_type=float_type)
        * score_scale
    )
    scores = jnp.where(allowed, raw, NEGATIVE)
    highest = jnp.max(scores, -1, keepdims=True)
    log_total = highest + jnp.log(jnp.sum(jnp.exp(scores - highest), -1, keepdims=True))
    prob_f = jnp.exp(scores - log_total)
    prob_b = prob_f.astype(half_type)
    mixed = (
        jnp.einsum("hqk,khd->qhd", prob_b, value_b, preferred_element_type=float_type)
        .astype(half_type)
        .reshape(seq_total, own_width)
    )
    proj_grad = rep_sum(contract_first(mixed, upstream))
    d_prob = jnp.einsum("qhd,khd->hqk", d_mixed_h, value_b, preferred_element_type=float_type)
    delta = jnp.sum(prob_f * d_prob, -1, keepdims=True)
    d_score = (prob_f * (d_prob - delta) * score_scale).astype(half_type)
    d_query = jnp.einsum("hqk,khd->qhd", d_score, keys_b, preferred_element_type=float_type)
    d_query = unrotate(d_query, cosine, sine).reshape(seq_total, own_width)
    d_keys = jnp.einsum("hqk,qhd->khd", d_score, query_b, preferred_element_type=float_type)
    d_keys = unrotate(d_keys, cosine, sine).reshape(seq_total, own_width)
    d_value = jnp.einsum("hqk,qhd->khd", prob_b, d_mixed_h, preferred_element_type=float_type)
    d_value = d_value.reshape(seq_total, own_width)

    d_own = jnp.concatenate([d_query, d_keys, d_value], 1).astype(half_type)
    qkv_group = jnp.zeros((seq_total, 3 * D), half_type)
    for step in range(group_size):
        block = d_own if step == 0 else shift(d_own, step)
        owner = (member - step) % group_size
        for i in range(3):
            qkv_group = lax.dynamic_update_slice_in_dim(
                qkv_group,
                block[:, i * own_width : (i + 1) * own_width],
                i * D + owner * own_width,
                1,
            )
    qkv_grad = rep_sum(contract_first(one_cols, qkv_group))
    d_one = contract_last(qkv_group, w_qkv)

    branch_whole = jnp.dot(mixed, w_out, preferred_element_type=float_type) + jnp.dot(
        act_b, w_fc2, preferred_element_type=float_type
    )
    branches = scatter_sum(lambda owner: rows_of(branch_whole, owner, tok_count))
    result = (tokens[0].astype(float_type) + branches + fc2_bias).astype(half_type)

    small = jnp.concatenate(
        [
            jnp.sum(d_one * normed_cols, 0),
            jnp.sum(d_one, 0),
            jnp.sum(d_two * normed_cols, 0),
            jnp.sum(d_two, 0),
            jnp.sum(d_query, 0),
            jnp.sum(d_value, 0),
            jnp.sum(columns_of(upstream, member, own_width).astype(float_type), 0),
            jnp.sum(d_hidden, 0),
        ]
    )
    small = lax.psum(small, "rep")
    pieces = [small[i * own_width : (i + 1) * own_width] for i in range(7)]

    scaled = d_one * gain_one + d_two * gain_two
    scaled_rows = jnp.zeros((tok_count, D), float_type)
    for step in range(group_size):
        block = rows_of(scaled, (member + step) % group_size, tok_count)
        if step > 0:
            block = shift(block, step)
        owner = (member - step) % group_size
        scaled_rows = lax.dynamic_update_slice_in_dim(scaled_rows, block, owner * own_width, 1)
    own_inputs = tokens[0].astype(float_type)
    own_centre = own_inputs - jnp.mean(own_inputs, -1, keepdims=True)
    own_rstd = lax.rsqrt(jnp.mean(own_centre * own_centre, -1, keepdims=True) + EPS)
    own_normed = own_centre * own_rstd
    grad_in = cotangent[0].astype(float_type) + own_rstd * (
        scaled_rows
        - jnp.mean(scaled_rows, -1, keepdims=True)
        - own_normed * jnp.mean(scaled_rows * own_normed, -1, keepdims=True)
    )
    return (
        result[None],
        grad_in[None],
        pieces[0],
        pieces[1],
        pieces[2],
        pieces[3],
        qkv_grad.astype(float_type),
        jnp.stack([pieces[4], pieces[5]]),
        proj_grad.astype(float_type),
        up_grad.astype(float_type),
        small[7 * own_width :],
        down_grad.astype(float_type),
        pieces[6],
    )


def solution(mesh):
    placed = (
        P("rep", "grp", None),
        P("rep", "grp", None),
        P("rep", None),
        P(),
        P(),
        P(),
        P(),
        P("grp", None),
        P(),
        P("grp", None),
        P("grp", None),
        P(),
        P("grp", None),
        P(),
    )
    return jax.shard_map(
        body,
        mesh=mesh,
        in_specs=placed,
        out_specs=(
            P("rep", "grp", None),
            P("rep", "grp", None),
            P("grp"),
            P("grp"),
            P("grp"),
            P("grp"),
            P("grp", None),
            P(None, "grp"),
            P("grp", None),
            P("grp", None),
            P("grp"),
            P("grp", None),
            P("grp"),
        ),
        check_vma=False,
    )
```
